128 devices in a mesh: dom: 8 (over y, core), grp: 16 (over z, x).
Axes of the slice: x: 4, y: 4, z: 4, core: 2. Of those that a mesh axis runs over, the one named last changes fastest.
Arguments:
- basis_values: bfloat16 [14336, 320, 256], P(('dom', 'grp')), may hold values from -0.47851562 to 0.47851562
- point_weights: float32 [14336, 256], P(('dom', 'grp')), may hold values from -6 to 6
- batch_blocks: int32 [14336, 5], P(('dom', 'grp')), may hold values from 0 to 31, as said below
- live_count: int32 [8, 16], P('dom', 'grp'), may hold values from 28 to 112, as said below
- dom_blocks: int32 [8, 32], replicated, may hold values from 0 to 255, as said below
- pair_mask: int32 [8, 32, 32], P('dom'), may hold values 0 or 1
Outputs:
- hamiltonian: float32 [16384, 16384], P('dom', 'grp')
The draws below stay inside these ranges and needn't reach their ends.
Inputs may be any that keep to these rules, and one draw needn't show every extreme that they name: `batch_blocks`: each batch names 5 different domain-local blocks. `dom_blocks`: the 32 blocks of a domain are different, and block p's global number is congruent to p modulo 16. Neighbouring domains share some blocks. `live_count`: some device holds 112 live batches in every draw, and some holds 28.
All inputs are finite; a program needn't handle non-finite values. No bound on the sum of `pair_mask` on one device may be relied on, other than what follows from the above.
Results may differ from the reference program's by a relative error of at most 0.0029.
Values sent between devices are 32-bit elements; how exact they have to be, the bound alone decides.
A program may use at most 128 MiB of HBM per device.

```python
import jax
import jax.numpy as jnp
from jax import lax

BLK = 64
NBLK = 256
NBT = 5
KB = 32
PTS = 256
BATCH_DEV = 112
NBAS = 16384
NFUN = 320
BATCHES = 14336
N_DOM = 8
N_GRP = 16


def draw_batch_blocks(key, part):
    scores = jax.random.randint(key, (BATCHES, KB), 0, 1 << 20) * KB + jnp.arange(KB, dtype=jnp.int32)[None, :]
    order = jnp.argsort(scores, axis=1)
    return order[:, :NBT].astype(jnp.int32)


def draw_dom_blocks(key, part):
    residue_span = NBLK // N_GRP
    domain = jnp.arange(N_DOM, dtype=jnp.int32)[:, None]
    local = jnp.arange(KB, dtype=jnp.int32)[None, :]
    residue = local % N_GRP
    level = local // N_GRP
    jitter = jax.random.randint(key, (N_DOM, KB), 0, 3)
    jitter = jitter.at[0, 0].set(1).at[0, N_GRP - 1].set(0)
    column = (domain * residue_span // N_DOM + 3 * level + jitter - 1 + residue_span) % residue_span
    return (residue + N_GRP * column).astype(jnp.int32)


def draw_live_count(key, part):
    first, second = jax.random.split(key)
    counts = jax.random.randint(first, (N_DOM * N_GRP,), BATCH_DEV // 4, BATCH_DEV + 1)
    where_full = jax.random.randint(second, (), 0, N_DOM * N_GRP)
    counts = counts.at[where_full].set(BATCH_DEV)
    counts = counts.at[(where_full + 1) % (N_DOM * N_GRP)].set(BATCH_DEV // 4)
    return counts.reshape(N_DOM, N_GRP).astype(jnp.int32)


def touch_ends(drawn, own_key, smallest, high):
    longest = drawn.shape.index(max(drawn.shape))
    spots = []
    for shift in (0, 1):
        where = [jax.random.randint(jax.random.fold_in(own_key, axis), (), 0, length) for axis, length in enumerate(drawn.shape)]
        where[longest] = (where[longest] + shift) % drawn.shape[longest]
        spots.append(tuple(where))
    return drawn.at[spots[0]].set(smallest).at[spots[1]].set(high)


def levels(key, dims, cuts, smallest, high):
    def one(position, blocks):
        draws = jax.random.uniform(jax.random.fold_in(jax.random.fold_in(key, 6), position), (blocks,), jnp.float32, smallest / len(cuts), high / len(cuts))
        return jnp.repeat(jnp.exp(draws), dims[position] // blocks).reshape((-1,) + (1,) * (len(dims) - position - 1))

    level = one(*cuts[0])
    for cut in cuts[1:]:
        level = level * one(*cut)
    return level


def normal_values(own_key, extent, deviation, reach, shards=(), kind=jnp.bfloat16):
    factor_of = levels(own_key, extent, shards, -0.22, 0.18) if shards else 1.0
    result = jax.random.normal(own_key, extent, jnp.float32) * deviation * factor_of
    return jnp.minimum(jnp.maximum(result, -reach), reach).astype(kind)


def setup_inputs(seed: int = 0) -> dict:
    splits = jax.random.split(jax.random.key(seed), 7)
    basis_values = normal_values(splits[0], (BATCHES, NFUN, PTS), 0.08, 0.47851562, ((0, 128),))
    point_weights = normal_values(splits[1], (BATCHES, PTS), 1.0, 6.0, ((0, 128),), jnp.float32)
    batch_blocks = draw_batch_blocks(jax.random.fold_in(splits[6], 71), 0)
    live_count = draw_live_count(jax.random.fold_in(splits[6], 71), 0)
    dom_blocks = draw_dom_blocks(jax.random.fold_in(splits[6], 71), 0)
    pair_mask = touch_ends((jax.random.randint(splits[5], (N_DOM, KB, KB), 0, 4) < 3).astype(jnp.int32), jax.random.fold_in(splits[5], 1), 0, 1)
    return {"basis_values": basis_values, "point_weights": point_weights, "batch_blocks": batch_blocks, "live_count": live_count, "dom_blocks": dom_blocks, "pair_mask": pair_mask}


def reference(basis_values, point_weights, batch_blocks, live_count, dom_blocks, pair_mask):
    per_domain = N_GRP * BATCH_DEV
    row_count = NBLK // N_DOM
    col_count = NBLK // N_GRP
    tile_size = BLK * BLK
    accum = jnp.zeros((NBLK * NBLK, tile_size), jnp.float32)
    for domain in range(N_DOM):
        def add_batch(number, partial_value):
            batch = (domain * per_domain + number).astype(jnp.int32)
            values = lax.dynamic_index_in_dim(basis_values, batch, 0, keepdims=False)
            weights = lax.dynamic_index_in_dim(point_weights, batch, 0, keepdims=False)
            device_slot = (number // BATCH_DEV).astype(jnp.int32)
            slot_index = number % BATCH_DEV
            alive = slot_index < live_count[domain][device_slot]
            weights = jnp.where(alive, weights, jnp.zeros_like(weights))
            scaled = (values.astype(jnp.float32) * weights[None, :]).astype(jnp.bfloat16)
            product = jnp.dot(values, scaled.T, preferred_element_type=jnp.float32)
            tiles = product.reshape(NBT, BLK, NBT, BLK).transpose(0, 2, 1, 3).reshape(NBT * NBT, tile_size)
            blocks = lax.dynamic_index_in_dim(batch_blocks, batch, 0, keepdims=False)
            targets = (blocks[:, None] * KB + blocks[None, :]).reshape(-1)
            return partial_value.at[targets].add(tiles)

        partial_value = lax.fori_loop(0, per_domain, add_batch, jnp.zeros((KB * KB, tile_size), jnp.float32))
        partial_value = partial_value * pair_mask[domain].reshape(-1)[:, None].astype(jnp.float32)
        block_ids = dom_blocks[domain]
        row_place = (block_ids % N_DOM) * row_count + block_ids // N_DOM
        col_place = (block_ids % N_GRP) * col_count + block_ids // N_GRP
        targets = (row_place[:, None] * NBLK + col_place[None, :]).reshape(-1)
        accum = accum.at[targets].add(partial_value)
    return accum.reshape(NBLK, NBLK, BLK, BLK).transpose(0, 2, 1, 3).reshape(NBAS, NBAS)
```

```python
import numpy as np
import jax
import jax.numpy as jnp
from jax import lax
from jax.experimental import pallas as pl
from jax.experimental.pallas import tpu as pltpu
from jax.sharding import PartitionSpec as P

SLOTS = 112
TILES = 272
UNROLL = 8
CHUNK = 8


def place_table():
    table = np.zeros((32, 16), np.int32)
    for key in range(32):
        a, h = key // 2, key % 2
        for b in range(16):
            d = abs(b - a)
            lo, hi = min(a, b), max(a, b)
            if d == 8:
                table[key, b] = 256 + (lo if h == 0 else hi)
            else:
                owner, delta = (hi, d) if d < 8 else (lo, 16 - d)
                table[key, b] = delta // 2 * 64 + owner * 4 + delta % 2 * 2 + h
    return table.reshape(-1)


def sort5(v):
    v = list(v)
    for i, j in ((0, 1), (3, 4), (2, 4), (2, 3), (1, 4), (0, 3), (0, 2), (1, 3), (1, 2)):
        low, high = jnp.minimum(v[i], v[j]), jnp.maximum(v[i], v[j])
        v[i], v[j] = low, high
    return v


def products_kernel(table, blocks, live, weights, basis, out, vbuf, acc, spad, sems, out_sem):
    count = live[0, 0]

    def load(c):
        return pltpu.make_async_copy(
            basis.at[pl.ds(c * CHUNK, CHUNK)], vbuf.at[pl.ds(c * CHUNK, CHUNK)], sems.at[c]
        )

    @pl.loop(0, SLOTS // CHUNK)
    def _(c):
        @pl.when(c * CHUNK < count)
        def _():
            load(c).start()

    @pl.loop(0, TILES, step=4)
    def _(n):
        for k in range(4):
            acc[n + k] = jnp.zeros((64, 128), jnp.float32)

    def batch(b, u):
        packed = []
        for i in range(5):
            p = blocks[b, i]
            packed.append((((p & 15) << 1) + (p >> 4)) * 8 + i)
        packed = sort5(packed)
        key = [v >> 3 for v in packed]
        half = [v & 1 for v in key]
        cls = [v >> 1 for v in key]
        row = [v << 4 for v in key]
        w = weights[pl.ds(b, 1), :] * jnp.where(b < count, 1.0, 0.0)
        values = []
        for i in range(5):
            v = vbuf[b, pl.ds(pl.multiple_of((packed[i] & 7) * 64, 64), 64), :]
            values.append(v)
            s = (v.astype(jnp.float32) * w).astype(jnp.bfloat16)
            spad[u, pl.ds(pl.multiple_of(i * 128 + half[i] * 64, 64), 64), :] = s
            spad[u, pl.ds(pl.multiple_of(i * 128 + 64 - half[i] * 64, 64), 64), :] = jnp.zeros_like(s)
        for first, cols in ((0, 2), (2, 2), (4, 1)):
            rows = first + cols
            lhs = jnp.concatenate(values[:rows], axis=0)
            rhs = spad[u, first * 128 : (first + cols) * 128, :]
            prod = lax.dot_general(lhs, rhs, (((1,), (1,)), ((), ())), preferred_element_type=jnp.float32)
            for c in range(cols):
                j = first + c
                spots, sums = [], []
                for i in range(j + 1):
                    spot = table[row[i] + cls[j]]
                    spots.append(spot)
                    sums.append(acc[spot] + prod[i * 64 : i * 64 + 64, c * 128 : c * 128 + 128])
                for spot, value in zip(spots, sums):
                    acc[spot] = value

    @pl.loop(0, pl.cdiv(count, UNROLL))
    def _(n):
        @pl.when(lax.rem(n * UNROLL, CHUNK) == 0)
        def _():
            load(n * UNROLL // CHUNK).wait()

        for u in range(UNROLL):
            batch(n * UNROLL + u, u)

    done = pltpu.make_async_copy(acc, out, out_sem)
    done.start()
    done.wait()


def products(basis_values, point_weights, batch_blocks, live_count):
    smem = pl.BlockSpec(memory_space=pltpu.SMEM)
    return pl.pallas_call(
        products_kernel,
        out_shape=jax.ShapeDtypeStruct((TILES, 64, 128), jnp.float32),
        in_specs=[smem, smem, smem, pl.BlockSpec(memory_space=pltpu.VMEM), pl.BlockSpec(memory_space=pl.ANY)],
        out_specs=pl.BlockSpec(memory_space=pl.ANY),
        scratch_shapes=[
            pltpu.VMEM((SLOTS, 320, 256), jnp.bfloat16),
            pltpu.VMEM((TILES, 64, 128), jnp.float32),
            pltpu.VMEM((UNROLL, 640, 256), jnp.bfloat16),
            pltpu.SemaphoreType.DMA((SLOTS // CHUNK,)),
            pltpu.SemaphoreType.DMA,
        ],
        compiler_params=pltpu.CompilerParams(vmem_limit_bytes=60 * 2**20),
        name="products",
    )(jnp.asarray(place_table()), batch_blocks, live_count, point_weights, basis_values)


MESH = pl.DeviceIdType.MESH
X_FIRST = (True, False, True, False, True, False)


def exchange_kernel(mask, partial, out, relay, direct, final, stage, relay2, direct2, final2, half_sum,
                    send, send_half, sem1, sem2, send1, send2, arrive, leave):
    dom, grp = lax.axis_index("dom"), lax.axis_index("grp")
    x, z = grp % 4, grp // 4

    def at(first, second, x_first):
        return second * 4 + first if x_first else first * 4 + second

    barrier = pltpu.get_barrier_semaphore()
    peers = [(dom, z * 4 + (x + 1) % 4), (dom, z * 4 + (x + 3) % 4),
             (dom, (z + 1) % 4 * 4 + x), (dom, (z + 3) % 4 * 4 + x)]
    peers += [((dom + n) % 8, grp) for n in range(1, 8)]
    source = (grp + 1 + (dom - grp - 1) % 8) % 16
    peers += [(n, source) for n in range(8)]
    for peer in peers:
        pl.semaphore_signal(barrier, inc=1, device_id=peer, device_id_type=MESH)
    pl.semaphore_wait(barrier, len(peers))

    def piece(k, owner, h):
        if k < 4:
            return partial.at[pl.ds(64 * k + 4 * owner + 2 * h, 2)]
        return partial.at[pl.ds(256 + owner, 1), pl.ds((k - 4) * 32 + 16 * h, 16), :]

    def view(buffers, k, *index):
        return buffers[k // 4].at[(k % 4, *index)]

    def remote(src, dst, send_sem, recv_sem, peer):
        return pltpu.make_async_remote_copy(src_ref=src, dst_ref=dst, send_sem=send_sem, recv_sem=recv_sem,
                                            device_id=peer, device_id_type=MESH)

    def copies1(k, s):
        xf = X_FIRST[k]
        mf = x if xf else z
        right, left, far = (mf + 1) % 4, (mf + 3) % 4, (mf + 2) % 4
        ms = z if xf else x
        so = (ms + s) % 4
        to_right = (dom, at(right, ms, xf))
        to_left = (dom, at(left, ms, xf))

        specs = [
            (piece(k, at(far, so, xf), 0), view(relay, k, s, 0), to_right),
            (piece(k, at(far, so, xf), 1), view(relay, k, s, 1), to_left),
            (piece(k, at(right, so, xf), 1), view(direct, k, s, 1), to_right),
            (piece(k, at(left, so, xf), 0), view(direct, k, s, 0), to_left),
            (view(relay, k, s, 0), view(final, k, s, 0), to_right),
            (view(relay, k, s, 1), view(final, k, s, 1), to_left),
        ]

        def copy(n):
            src, dst, peer = specs[n]
            return remote(src, dst, send1.at[k, s, n], sem1.at[k, s, n], peer)

        return copy, (right, left, mf, so, xf)

    def copies2(k):
        xf = X_FIRST[k]
        mf, ms = (x, z) if xf else (z, x)
        to_right = (dom, at(mf, (ms + 1) % 4, xf))
        to_left = (dom, at(mf, (ms + 3) % 4, xf))

        specs = [
            (view(stage, k, 2, 0), view(relay2, k, 0), to_right),
            (view(stage, k, 2, 1), view(relay2, k, 1), to_left),
            (view(stage, k, 1, 1), view(direct2, k, 1), to_right),
            (view(stage, k, 3, 0), view(direct2, k, 0), to_left),
            (view(relay2, k, 0), view(final2, k, 0), to_right),
            (view(relay2, k, 1), view(final2, k, 1), to_left),
        ]

        def copy(n):
            src, dst, peer = specs[n]
            return remote(src, dst, send2.at[k, n], sem2.at[k, n], peer)

        return copy

    ORDER = (2, 1, 3, 0)

    def begin(ks):
        for s in ORDER:
            for k in ks:
                c, _ = copies1(k, s)
                c(0).start()
                c(1).start()
        for s in ORDER:
            for k in ks:
                c, _ = copies1(k, s)
                c(2).start()
                c(3).start()

    def pass_on(ks):
        for s in ORDER:
            for k in ks:
                c, (right, left, mf, so, xf) = copies1(k, s)
                for h, owner in ((0, right), (1, left)):
                    c(h).wait_recv()
                    slot = view(relay, k, s, h)
                    slot[...] = slot[...] + piece(k, at(owner, so, xf), h)[...]
                    c(4 + h).start()

    def settle(ks):
        for s in ORDER:
            for k in ks:
                c, (right, left, mf, so, xf) = copies1(k, s)
                for h in (0, 1):
                    c(4 + h).wait_recv()
                    c(3 - h).wait_recv()
                    view(stage, k, s, h)[...] = (
                        piece(k, at(mf, so, xf), h)[...] + view(final, k, s, h)[...] + view(direct, k, s, h)[...]
                    )
            for k in ks:
                c = copies2(k)
                if s == 2:
                    c(0).start()
                    c(1).start()
                if s == 1:
                    c(2).start()
                if s == 3:
                    c(3).start()

    def pass_on2(ks):
        for k in ks:
            c = copies2(k)
            for h, s in ((0, 1), (1, 3)):
                c(h).wait_recv()
                slot = view(relay2, k, h)
                slot[...] = slot[...] + view(stage, k, s, h)[...]
                c(4 + h).start()

    def settle2(ks):
        for k in ks:
            c = copies2(k)
            for h in (0, 1):
                c(4 + h).wait_recv()
                c(3 - h).wait_recv()
                value = view(stage, k, 0, h)[...] + view(final2, k, h)[...] + view(direct2, k, h)[...]
                if k < 4:
                    hand_out(2 * k + h, value.reshape(128, 128))
                else:
                    half_sum[(k - 4) * 32 + 16 * h : (k - 4) * 32 + 16 * h + 16, :] = value[0]

    lane = lax.broadcasted_iota(jnp.int32, (64, 128), 1)
    low_half = lax.broadcasted_iota(jnp.int32, (128, 128), 1) < 64
    top_half = lax.broadcasted_iota(jnp.int32, (128, 128), 0) < 64

    def factor(p, q):
        return mask[0, p, q].astype(jnp.float32)

    def kept(row, col):
        halves = [jnp.where(lane < 64, factor(row + 16 * i, col), factor(row + 16 * i, col + 16)) for i in (0, 1)]
        return jnp.concatenate(halves, axis=0)

    def to_group(src, a, rows, n):
        target = a % 8
        dst = out.at[dom, a // 8, rows]

        @pl.when(target != dom)
        def _():
            remote(src, dst, leave.at[0, n], arrive.at[dom, a // 8], (target, grp)).start()

        @pl.when(target == dom)
        def _():
            pltpu.make_async_copy(src, dst, arrive.at[dom, a // 8]).start()

    def to_other(src, a, rows, n):
        dst = out.at[dom, grp // 8, rows]
        return remote(src, dst, leave.at[1, n], arrive.at[dom, grp // 8], (grp % 8, a))

    whole = pl.ds(0, 128)

    def hand_out(n, value):
        a = (grp + 16 - n) % 16
        turned = value.T
        if n == 0:
            send[0, 0] = jnp.where(top_half | ~low_half, value, turned) * kept(a, grp)
            to_group(send.at[0, 0], a, whole, 0)
            return
        wrapped = grp < n
        send[0, n] = jnp.where(wrapped, turned, value) * kept(a, grp)
        to_group(send.at[0, n], a, whole, n)
        send[1, n] = jnp.where(wrapped, value, turned) * kept(grp, a)
        to_other(send.at[1, n], a, whole, n).start()

    def hand_out_half():
        a = (grp + 8) % 16
        h = grp // 8
        low, high = grp % 8, grp % 8 + 8
        value = half_sum[...]
        upper = value * jnp.where(lane < 64, factor(low + 16 * h, high), factor(low + 16 * h, high + 16))
        lower = value * jnp.where(lane < 64, factor(high, low + 16 * h), factor(high + 16, low + 16 * h))
        rows = pl.ds(pl.multiple_of(h * 64, 64), 64)
        send_half[0] = jnp.where(h == 0, lower, upper)
        to_group(send_half.at[0], a, rows, 8)
        send_half[1] = jnp.where(h == 0, upper, lower)
        to_other(send_half.at[1], a, rows, 8).start()

    first, last = (0, 1), (4, 5, 2, 3)
    begin(first)
    pass_on(first)
    begin(last)
    settle(first)
    pass_on(last)
    pass_on2(first)
    settle2(first)
    settle(last)
    pass_on2(last)
    settle2(last)
    hand_out_half()

    for k in range(6):
        for s in range(4):
            for n in range(6):
                copies1(k, s)[0](n).wait_send()
        for n in range(6):
            copies2(k)(n).wait_send()
    for n in range(9):
        a = (grp + 16 - n) % 16
        src = send_half if n == 8 else send.at[:, n]
        rows = pl.ds(0, 64) if n == 8 else whole

        @pl.when(a % 8 != dom)
        def _():
            remote(src.at[0], out.at[dom, a // 8, rows], leave.at[0, n], arrive.at[dom, a // 8], (a % 8, grp)).wait_send()

        if n:
            to_other(src.at[1], a, rows, n).wait_send()
    for d in range(8):
        for t in range(2):
            pltpu.make_async_copy(out.at[d, t], out.at[d, t], arrive.at[d, t]).wait()


def exchange(partial, pair_mask):
    def pair(*lead):
        return [pltpu.VMEM((4, *lead, 2, 64, 128), jnp.float32), pltpu.VMEM((2, *lead, 1, 16, 128), jnp.float32)]

    buffers = [pair(4, 2), pair(4, 2), pair(4, 2), pair(4, 2), pair(2), pair(2), pair(2)]
    flat = [b for two in buffers for b in two]
    rest = [
        pltpu.VMEM((64, 128), jnp.float32),
        pltpu.VMEM((2, 8, 128, 128), jnp.float32),
        pltpu.VMEM((2, 64, 128), jnp.float32),
        pltpu.SemaphoreType.DMA((6, 4, 6)),
        pltpu.SemaphoreType.DMA((6, 6)),
        pltpu.SemaphoreType.DMA((6, 4, 6)),
        pltpu.SemaphoreType.DMA((6, 6)),
        pltpu.SemaphoreType.DMA((8, 2)),
        pltpu.SemaphoreType.DMA((2, 9)),
    ]

    def body(mask, partial, out, *refs):
        pairs = [refs[2 * n : 2 * n + 2] for n in range(7)]
        exchange_kernel(mask, partial, out, *pairs, *refs[14:])

    return pl.pallas_call(
        body,
        out_shape=jax.ShapeDtypeStruct((8, 2, 128, 128), jnp.float32),
        in_specs=[pl.BlockSpec(memory_space=pltpu.SMEM), pl.BlockSpec(memory_space=pltpu.VMEM)],
        out_specs=pl.BlockSpec(memory_space=pl.ANY),
        scratch_shapes=flat + rest,
        compiler_params=pltpu.CompilerParams(
            collective_id=0, has_side_effects=True, vmem_limit_bytes=48 * 2**20
        ),
        name="exchange",
    )(pair_mask, partial)


def place_kernel(ids, tiles, out, image, sem):
    dom, grp = lax.axis_index("dom"), lax.axis_index("grp")

    @pl.loop(0, 2048, step=64)
    def _(n):
        image[pl.ds(pl.multiple_of(n, 64), 64), :] = jnp.zeros((64, 1024), jnp.float32)

    left = lax.broadcasted_iota(jnp.int32, (64, 128), 1) < 64

    @pl.loop(0, 8)
    def _(d):
        for t in range(2):
            quad = tiles[d, t]
            if t == 1:
                turn = jnp.logical_and(grp < 8, dom == grp)
                quad = jnp.where(turn, quad.T, quad)
            for i in range(2):
                row = ids[d, dom + 8 * t + 16 * i] // 8
                part = quad[64 * i : 64 * i + 64]
                other = jnp.concatenate([part[:, 64:], part[:, :64]], axis=1)
                for j in range(2):
                    col = ids[d, grp + 16 * j] // 16
                    half = col % 2
                    value = jnp.where(half == j, part, other)
                    value = jnp.where(left == (half == 0), value, 0.0)
                    spot = (pl.ds(pl.multiple_of(row * 64, 64), 64), pl.ds(pl.multiple_of(col // 2 * 128, 128), 128))
                    image[spot] = image[spot] + value

    done = pltpu.make_async_copy(image, out, sem)
    done.start()
    done.wait()


def place(dom_blocks, tiles):
    return pl.pallas_call(
        place_kernel,
        out_shape=jax.ShapeDtypeStruct((2048, 1024), jnp.float32),
        in_specs=[pl.BlockSpec(memory_space=pltpu.SMEM), pl.BlockSpec(memory_space=pltpu.VMEM)],
        out_specs=pl.BlockSpec(memory_space=pl.ANY),
        scratch_shapes=[pltpu.VMEM((2048, 1024), jnp.float32), pltpu.SemaphoreType.DMA],
        compiler_params=pltpu.CompilerParams(vmem_limit_bytes=24 * 2**20),
        name="place",
    )(dom_blocks, tiles)


def local(basis_values, point_weights, batch_blocks, live_count, dom_blocks, pair_mask):
    partial = products(basis_values, point_weights, batch_blocks, live_count)
    tiles = exchange(partial, pair_mask)
    return place(dom_blocks, tiles)


def solution(mesh):
    return jax.shard_map(
        local,
        mesh=mesh,
        in_specs=(
            P(("dom", "grp"), None, None),
            P(("dom", "grp"), None),
            P(("dom", "grp"), None),
            P("dom", "grp"),
            P(),
            P("dom", None, None),
        ),
        out_specs=P("dom", "grp"),
        check_vma=False,
    )
```

```python
import numpy as np
import jax
import jax.numpy as jnp
from jax import lax
from jax.experimental import pallas as pl
from jax.experimental.pallas import tpu as pltpu
from jax.sharding import PartitionSpec as P

SLOTS = 112
TILES = 272
UNROLL = 8
CHUNK = 8


SLABS = ((True, (1, 8), (2,)), (False, (3,), (4,)), (True, (5,), (6,)), (False, (7,), (0,)))
SIZES = tuple(tuple(sum(1 if q == 8 else 2 for q in half) for half in slab[1:]) for slab in SLABS)
ROUNDS = ((0, 1), (2, 3))
BASES = tuple(16 * sum(sum(n) for n in SIZES[:k]) for k in range(len(SLABS)))
X_FIRST = tuple(slab[0] for slab in SLABS)


def place_table():
    table = np.zeros((32, 16), np.int32)
    for key in range(32):
        a, h = key // 2, key % 2
        for b in range(16):
            d = abs(b - a)
            lo, hi = min(a, b), max(a, b)
            owner, delta = (hi, d) if d < 8 else (lo, 16 - d)
            if d == 8:
                owner = hi if h else lo
            for k, slab in enumerate(SLABS):
                quads = slab[1] + slab[2]
                if delta in quads:
                    ahead = sum(1 if q == 8 else 2 for q in quads[: quads.index(delta)])
                    table[key, b] = BASES[k] + owner * sum(SIZES[k]) + ahead + (0 if d == 8 else h)
    return table.reshape(-1)


def sort5(v):
    v = list(v)
    for i, j in ((0, 1), (3, 4), (2, 4), (2, 3), (1, 4), (0, 3), (0, 2), (1, 3), (1, 2)):
        low, high = jnp.minimum(v[i], v[j]), jnp.maximum(v[i], v[j])
        v[i], v[j] = low, high
    return v


def products_kernel(table, blocks, live, weights, basis, out, vbuf, acc, scaled, corner, sems):
    count = live[0, 0]

    def load(c):
        return pltpu.make_async_copy(
            basis.at[pl.ds(c * CHUNK, CHUNK)], vbuf.at[pl.ds(c * CHUNK, CHUNK)], sems.at[c]
        )

    @pl.loop(0, SLOTS // CHUNK)
    def _(c):
        @pl.when(c * CHUNK < count)
        def _():
            load(c).start()

    @pl.loop(0, 2 * TILES, step=16)
    def _(n):
        for k in range(16):
            acc[n + k] = jnp.zeros((64, 128), jnp.float32)

    left = lax.broadcasted_iota(jnp.int32, (64, 128), 1) < 64

    def dot(lhs, rhs):
        return lax.dot_general(lhs, rhs, (((1,), (1,)), ((), ())), preferred_element_type=jnp.float32)

    def add(spots, parts):
        sums = [acc[spot] + part for spot, part in zip(spots, parts)]
        for spot, value in zip(spots, sums):
            acc[spot] = value

    def half_of(prod, row, col):
        part = prod[row * 64 : row * 64 + 64, col // 2 * 128 : col // 2 * 128 + 128]
        return jnp.where(left == (col % 2 == 0), part, 0.0)

    def spot_of(key_i, key_j, col):
        return table[key_i * 16 + (key_j >> 1)] + ((key_j & 1) ^ (col % 2)) * TILES

    def prepare(b, u):
        packed = []
        for i in range(5):
            p = blocks[i, b]
            packed.append((((p & 15) << 1) + (p >> 4)) * 8 + i)
        packed = sort5(packed)
        w = weights[pl.ds(b, 1), :] * jnp.where(b < count, 1.0, 0.0)
        values = []
        for i in range(5):
            v = vbuf[b, pl.ds(pl.multiple_of((packed[i] & 7) * 64, 64), 64), :]
            values.append(v)
            s = (v.astype(jnp.float32) * w).astype(jnp.bfloat16)
            if i:
                scaled[u, i * 64 - 64 : i * 64, :] = s
            else:
                corner[u // 4, u % 4 * 64 : u % 4 * 64 + 64, :] = s
        return [v >> 3 for v in packed], values

    def batch(u, key, values):
        prod = dot(jnp.concatenate(values, axis=0), scaled[u])
        for j in range(1, 5):
            add([spot_of(key[i], key[j], j - 1) for i in range(j + 1)], [half_of(prod, i, j - 1) for i in range(j + 1)])

    def corners(g, keys, values):
        prod = dot(jnp.concatenate(values, axis=0), corner[g])
        for c in range(4):
            add([spot_of(keys[c], keys[c], c)], [half_of(prod, c, c)])

    @pl.loop(0, pl.cdiv(count, UNROLL))
    def _(n):
        @pl.when(lax.rem(n * UNROLL, CHUNK) == 0)
        def _():
            load(n * UNROLL // CHUNK).wait()

        for g in range(UNROLL // 4):
            firsts = []
            for u in range(4 * g, 4 * g + 4):
                key, values = prepare(n * UNROLL + u, u)
                firsts.append((key[0], values[0]))
                batch(u, key, values)
            corners(g, [f[0] for f in firsts], [f[1] for f in firsts])

    @pl.loop(0, TILES, step=16)
    def _(n):
        for k in range(16):
            out[n + k] = acc[n + k] + pltpu.roll(acc[n + k + TILES], 64, 1)


def products(basis_values, point_weights, batch_blocks, live_count):
    smem = pl.BlockSpec(memory_space=pltpu.SMEM)
    return pl.pallas_call(
        products_kernel,
        out_shape=jax.ShapeDtypeStruct((TILES, 64, 128), jnp.float32),
        in_specs=[smem, smem, smem, pl.BlockSpec(memory_space=pltpu.VMEM), pl.BlockSpec(memory_space=pl.ANY)],
        out_specs=pl.BlockSpec(memory_space=pltpu.VMEM),
        scratch_shapes=[
            pltpu.VMEM((SLOTS, 320, 256), jnp.bfloat16),
            pltpu.VMEM((2 * TILES, 64, 128), jnp.float32),
            pltpu.VMEM((UNROLL, 256, 256), jnp.bfloat16),
            pltpu.VMEM((UNROLL // 4, 256, 256), jnp.bfloat16),
            pltpu.SemaphoreType.DMA((SLOTS // CHUNK,)),
        ],
        compiler_params=pltpu.CompilerParams(vmem_limit_bytes=40 * 2**20),
        name="products",
    )(jnp.asarray(place_table()), batch_blocks.T, live_count, point_weights, basis_values)


MESH = pl.DeviceIdType.MESH

def exchange_kernel(mask, partial, out, relay, direct, final, stage, relay2, direct2, final2,
                    send, send_half, pass_by, sem1, sem2, send1, send2, arrive, leave, passing, sweeps):
    dom, grp = lax.axis_index("dom"), lax.axis_index("grp")
    x, z = grp % 4, grp // 4

    def at(first, second, x_first):
        return second * 4 + first if x_first else first * 4 + second

    x_near = [(dom, at((x + n) % 4, z, True)) for n in (1, 3)]
    z_near = [(dom, at(x, (z + n) % 4, True)) for n in (1, 3)]
    y_near = [((dom + n) % 8, grp) for n in (2, 6)]
    core_near = [(dom // 2 * 2 + 1 - dom % 2, grp)]

    def signal(sem, peers):
        for peer in peers:
            pl.semaphore_signal(sem, inc=1, device_id=peer, device_id_type=MESH)

    barrier = pltpu.get_barrier_semaphore()
    everyone = x_near + z_near + y_near + core_near
    signal(barrier, everyone)
    pl.semaphore_wait(barrier, len(everyone))
    todo = [x_near, z_near, z_near, y_near, y_near, core_near]

    def sweep():
        if todo:
            n = 6 - len(todo)
            peers = todo.pop(0)
            signal(sweeps.at[n], peers)
            pl.semaphore_wait(sweeps.at[n], len(peers))

    def piece(k, owner, h):
        return partial.at[pl.ds(BASES[k] + sum(SIZES[k]) * owner + h * SIZES[k][0], SIZES[k][h])]

    def view(buffers, k, *index):
        return buffers[k].at[(*index, pl.ds(0, SIZES[k][index[-1]]))]

    def remote(src, dst, send_sem, recv_sem, peer):
        return pltpu.make_async_remote_copy(src_ref=src, dst_ref=dst, send_sem=send_sem, recv_sem=recv_sem,
                                            device_id=peer, device_id_type=MESH)

    def copies1(k, s):
        xf = X_FIRST[k]
        mf = x if xf else z
        right, left, far = (mf + 1) % 4, (mf + 3) % 4, (mf + 2) % 4
        ms = z if xf else x
        so = (ms + s) % 4
        to_right = (dom, at(right, ms, xf))
        to_left = (dom, at(left, ms, xf))

        specs = [
            (piece(k, at(far, so, xf), 0), view(relay, k, s, 0), to_right),
            (piece(k, at(far, so, xf), 1), view(relay, k, s, 1), to_left),
            (piece(k, at(right, so, xf), 1), view(direct, k, s, 1), to_right),
            (piece(k, at(left, so, xf), 0), view(direct, k, s, 0), to_left),
            (view(relay, k, s, 0), view(final, k, s, 0), to_right),
            (view(relay, k, s, 1), view(final, k, s, 1), to_left),
        ]

        def copy(n):
            src, dst, peer = specs[n]
            return remote(src, dst, send1.at[k, s, n], sem1.at[k, s, n], peer)

        return copy, (right, left, mf, so, xf)

    def copies2(k):
        xf = X_FIRST[k]
        mf, ms = (x, z) if xf else (z, x)
        to_right = (dom, at(mf, (ms + 1) % 4, xf))
        to_left = (dom, at(mf, (ms + 3) % 4, xf))

        specs = [
            (view(stage, k, 2, 0), view(relay2, k, 0), to_right),
            (view(stage, k, 2, 1), view(relay2, k, 1), to_left),
            (view(stage, k, 1, 1), view(direct2, k, 1), to_right),
            (view(stage, k, 3, 0), view(direct2, k, 0), to_left),
            (view(relay2, k, 0), view(final2, k, 0), to_right),
            (view(relay2, k, 1), view(final2, k, 1), to_left),
        ]

        def copy(n):
            src, dst, peer = specs[n]
            return remote(src, dst, send2.at[k, n], sem2.at[k, n], peer)

        return copy

    ORDER = (2, 1, 3, 0)
    items = [(r, s) for r in range(len(ROUNDS)) for s in ORDER]

    def begin(r, s):
        for kinds in ((0, 1), (2, 3)):
            for k in ROUNDS[r]:
                c, _ = copies1(k, s)
                for n in kinds:
                    c(n).start()

    def pass_on(r, s):
        for k in ROUNDS[r]:
            c, (right, left, mf, so, xf) = copies1(k, s)
            for h, owner in ((0, right), (1, left)):
                c(h).wait_recv()
                slot = view(relay, k, s, h)
                slot[...] = slot[...] + piece(k, at(owner, so, xf), h)[...]
                c(4 + h).start()

    def settle(r, s):
        for k in ROUNDS[r]:
            c, (right, left, mf, so, xf) = copies1(k, s)
            for h in (0, 1):
                c(4 + h).wait_recv()
                c(3 - h).wait_recv()
                view(stage, k, s, h)[...] = (
                    piece(k, at(mf, so, xf), h)[...] + view(final, k, s, h)[...] + view(direct, k, s, h)[...]
                )
            for n in {2: (0, 1), 1: (2,), 3: (3,), 0: ()}[s]:
                copies2(k)(n).start()

    def pass_on2(r):
        for k in ROUNDS[r]:
            c = copies2(k)
            for h, s in ((0, 1), (1, 3)):
                c(h).wait_recv()
                slot = view(relay2, k, h)
                slot[...] = slot[...] + view(stage, k, s, h)[...]
                c(4 + h).start()

    def settle2(r):
        for k in ROUNDS[r]:
            c = copies2(k)
            for h in (0, 1):
                c(4 + h).wait_recv()
                c(3 - h).wait_recv()
                value = view(stage, k, 0, h)[...] + view(final2, k, h)[...] + view(direct2, k, h)[...]
                ahead = 0
                for q in SLABS[k][1 + h]:
                    if q == 8:
                        hand_out_half(value[ahead])
                        ahead += 1
                    else:
                        hand_out(q, value[ahead : ahead + 2].reshape(128, 128))
                        ahead += 2

    lane = lax.broadcasted_iota(jnp.int32, (64, 128), 1)
    low_half = lax.broadcasted_iota(jnp.int32, (128, 128), 1) < 64
    top_half = lax.broadcasted_iota(jnp.int32, (128, 128), 0) < 64

    def factor(p, q):
        return mask[0, p, q].astype(jnp.float32)

    def kept(row, col):
        halves = [jnp.where(lane < 64, factor(row + 16 * i, col), factor(row + 16 * i, col + 16)) for i in (0, 1)]
        return jnp.concatenate(halves, axis=0)

    def to_group(src, a, rows, n):
        target = a % 8
        dst = out.at[dom, a // 8, rows]

        @pl.when(target != dom)
        def _():
            remote(src, dst, leave.at[0, n], arrive.at[dom, a // 8], (target, grp)).start()

        @pl.when(target == dom)
        def _():
            pltpu.make_async_copy(src, dst, arrive.at[dom, a // 8]).start()

    def to_other(src, a, rows, n):
        return remote(src, pass_by.at[n, rows], leave.at[1, n], passing.at[n], (dom, a))

    def forward(n):
        g = (grp + n) % 16
        rows = pl.ds(pl.multiple_of(g // 8 * 64, 64), 64) if n == 8 else whole
        to_other(pass_by.at[n, rows], g, rows, n).wait_recv()
        target = g % 8
        src, dst = pass_by.at[n, rows], out.at[dom, g // 8, rows]

        @pl.when(target != dom)
        def _():
            remote(src, dst, leave.at[2, n], arrive.at[dom, g // 8], (target, grp)).start()

        @pl.when(target == dom)
        def _():
            pltpu.make_async_copy(src, dst, arrive.at[dom, g // 8]).start()

    def forward_round(r):
        for k in ROUNDS[r]:
            for q in SLABS[k][1] + SLABS[k][2]:
                if q:
                    forward(q)

    whole = pl.ds(0, 128)

    def hand_out(n, value):
        a = (grp + 16 - n) % 16
        turned = value.T
        if n == 0:
            send[0, 0] = jnp.where(top_half | ~low_half, value, turned) * kept(a, grp)
            to_group(send.at[0, 0], a, whole, 0)
            return
        wrapped = grp < n
        send[0, n] = jnp.where(wrapped, turned, value) * kept(a, grp)
        to_group(send.at[0, n], a, whole, n)
        send[1, n] = jnp.where(wrapped, value, turned) * kept(grp, a)
        to_other(send.at[1, n], a, whole, n).start()

    def hand_out_half(value):
        a = (grp + 8) % 16
        h = grp // 8
        low, high = grp % 8, grp % 8 + 8
        upper = value * jnp.where(lane < 64, factor(low + 16 * h, high), factor(low + 16 * h, high + 16))
        lower = value * jnp.where(lane < 64, factor(high, low + 16 * h), factor(high + 16, low + 16 * h))
        rows = pl.ds(pl.multiple_of(h * 64, 64), 64)
        send_half[0] = jnp.where(h == 0, lower, upper)
        to_group(send_half.at[0], a, rows, 8)
        send_half[1] = jnp.where(h == 0, upper, lower)
        to_other(send_half.at[1], a, rows, 8).start()

    begin(*items[0])
    for i, (r, s) in enumerate(items):
        if i + 1 < len(items):
            begin(*items[i + 1])
        pass_on(r, s)
        if i:
            settle(*items[i - 1])
        sweep()
        if r and s == 2:
            pass_on2(r - 1)
        if r and s == 3:
            settle2(r - 1)
        if r > 1 and s == 2:
            forward_round(r - 2)
    settle(*items[-1])
    pass_on2(len(ROUNDS) - 1)
    forward_round(len(ROUNDS) - 2)
    settle2(len(ROUNDS) - 1)
    forward_round(len(ROUNDS) - 1)

    for k in range(len(SLABS)):
        for s in range(4):
            for n in range(6):
                copies1(k, s)[0](n).wait_send()
        for n in range(6):
            copies2(k)(n).wait_send()
    for n in range(9):
        a = (grp + 16 - n) % 16
        src = send_half if n == 8 else send.at[:, n]
        rows = pl.ds(0, 64) if n == 8 else whole

        @pl.when(a % 8 != dom)
        def _():
            remote(src.at[0], out.at[dom, a // 8, rows], leave.at[0, n], arrive.at[dom, a // 8], (a % 8, grp)).wait_send()

        if n:
            to_other(src.at[1], a, rows, n).wait_send()
            g = (grp + n) % 16

            @pl.when(g % 8 != dom)
            def _():
                remote(src.at[1], out.at[dom, g // 8, rows], leave.at[2, n], arrive.at[dom, g // 8],
                       (g % 8, grp)).wait_send()
    for d in range(8):
        for t in range(2):
            pltpu.make_async_copy(out.at[d, t], out.at[d, t], arrive.at[d, t]).wait()


def exchange(partial, pair_mask):
    count = len(SLABS)

    def per_slab(*lead):
        return [pltpu.VMEM((*lead, max(n), 64, 128), jnp.float32) for n in SIZES]

    flat = [b for lead in ((4, 2),) * 4 + ((2,),) * 3 for b in per_slab(*lead)]
    rest = [
        pltpu.VMEM((2, 8, 128, 128), jnp.float32),
        pltpu.VMEM((2, 64, 128), jnp.float32),
        pltpu.VMEM((9, 128, 128), jnp.float32),
        pltpu.SemaphoreType.DMA((count, 4, 6)),
        pltpu.SemaphoreType.DMA((count, 6)),
        pltpu.SemaphoreType.DMA((count, 4, 6)),
        pltpu.SemaphoreType.DMA((count, 6)),
        pltpu.SemaphoreType.DMA((8, 2)),
        pltpu.SemaphoreType.DMA((3, 9)),
        pltpu.SemaphoreType.DMA((9,)),
        pltpu.SemaphoreType.REGULAR((6,)),
    ]

    def body(mask, partial, out, *refs):
        groups = [refs[count * n : count * n + count] for n in range(7)]
        exchange_kernel(mask, partial, out, *groups, *refs[7 * count :])

    return pl.pallas_call(
        body,
        out_shape=jax.ShapeDtypeStruct((8, 2, 128, 128), jnp.float32),
        in_specs=[pl.BlockSpec(memory_space=pltpu.SMEM), pl.BlockSpec(memory_space=pltpu.VMEM)],
        out_specs=pl.BlockSpec(memory_space=pl.ANY),
        scratch_shapes=flat + rest,
        compiler_params=pltpu.CompilerParams(
            collective_id=0, has_side_effects=True, vmem_limit_bytes=26 * 2**20
        ),
        name="exchange",
    )(pair_mask, partial)


def place_kernel(ids, tiles, out, image, sem):
    dom, grp = lax.axis_index("dom"), lax.axis_index("grp")

    @pl.loop(0, 2048, step=64)
    def _(n):
        image[pl.ds(pl.multiple_of(n, 64), 64), :] = jnp.zeros((64, 1024), jnp.float32)

    left = lax.broadcasted_iota(jnp.int32, (64, 128), 1) < 64

    @pl.loop(0, 8)
    def _(d):
        for t in range(2):
            quad = tiles[d, t]
            if t == 1:
                turn = jnp.logical_and(grp < 8, dom == grp)
                quad = jnp.where(turn, quad.T, quad)
            for i in range(2):
                row = ids[d, dom + 8 * t + 16 * i] // 8
                part = quad[64 * i : 64 * i + 64]
                other = jnp.concatenate([part[:, 64:], part[:, :64]], axis=1)
                for j in range(2):
                    col = ids[d, grp + 16 * j] // 16
                    half = col % 2
                    value = jnp.where(half == j, part, other)
                    value = jnp.where(left == (half == 0), value, 0.0)
                    spot = (pl.ds(pl.multiple_of(row * 64, 64), 64), pl.ds(pl.multiple_of(col // 2 * 128, 128), 128))
                    image[spot] = image[spot] + value

    done = pltpu.make_async_copy(image, out, sem)
    done.start()
    done.wait()


def place(dom_blocks, tiles):
    return pl.pallas_call(
        place_kernel,
        out_shape=jax.ShapeDtypeStruct((2048, 1024), jnp.float32),
        in_specs=[pl.BlockSpec(memory_space=pltpu.SMEM), pl.BlockSpec(memory_space=pltpu.VMEM)],
        out_specs=pl.BlockSpec(memory_space=pl.ANY),
        scratch_shapes=[pltpu.VMEM((2048, 1024), jnp.float32), pltpu.SemaphoreType.DMA],
        compiler_params=pltpu.CompilerParams(vmem_limit_bytes=24 * 2**20),
        name="place",
    )(dom_blocks, tiles)


def local(basis_values, point_weights, batch_blocks, live_count, dom_blocks, pair_mask):
    partial = products(basis_values, point_weights, batch_blocks, live_count)
    tiles = exchange(partial, pair_mask)
    return place(dom_blocks, tiles)


def solution(mesh):
    return jax.shard_map(
        local,
        mesh=mesh,
        in_specs=(
            P(("dom", "grp"), None, None),
            P(("dom", "grp"), None),
            P(("dom", "grp"), None),
            P("dom", "grp"),
            P(),
            P("dom", None, None),
        ),
        out_specs=P("dom", "grp"),
        check_vma=False,
    )
```
